32 devices in a mesh: groups: 2 (over y), dp: 4 (over z), section: 4 (over x, core).
Axes of the slice: x: 2, y: 2, z: 4, core: 2. Of those that a mesh axis runs over, the one named last changes fastest.
Arguments:
- activations: bfloat16 [4, 32, 16, 16, 512], P('section', ('groups', 'dp')), parts along dimension 1, may hold values from -6 to 6
- depth_small: float32 [4, 3, 3, 512], P('section'), may hold values from -2 to 2
- point_first: bfloat16 [4, 512, 512], P('section'), may hold values from -0.25 to 0.25
- depth_large: float32 [4, 5, 5, 512], P('section'), may hold values from -1.25 to 1.25
- point_second: bfloat16 [4, 512, 512], P('section'), may hold values from -0.25 to 0.25
- head_weight: bfloat16 [1000, 512], replicated, may hold values from -0.25 to 0.25
- offsets: int32 [32], P(('groups', 'dp')), parts along dimension 0, may hold values from 0 to 15
- labels: int32 [32], P(('groups', 'dp')), parts along dimension 0, may hold values from 0 to 999
Outputs:
- grad_first: float32 [4, 1024, 512], P('section', 'groups'), parts along dimension 1
- grad_second: float32 [4, 1024, 512], P('section', 'groups'), parts along dimension 1
- grad_small: float32 [4, 6, 3, 512], P('section', 'groups'), parts along dimension 1
- grad_large: float32 [4, 10, 5, 512], P('section', 'groups'), parts along dimension 1
The draws below stay inside these ranges and needn't reach their ends.
There are 2 independent parts, one for each index of `groups`. The reference program is written for one: setup_inputs(seed, part) draws one part's arguments, and reference() takes and returns one part's arrays. A program takes and returns all parts, laid end to end along the dimension named above; an argument that names none is the same for every part. Nothing has to cross between parts.
All inputs are finite; a program needn't handle non-finite values.
Results may differ from the reference program's by a relative error of at most 0.0028.
Values may be sent and summed in bfloat16 or wider, within the bound.
A program may use at most 64 MiB of HBM per device.

```python
import jax
import jax.numpy as jnp
from jax import lax

CHANNELS = 512
CLASSES = 1000
HEIGHT = 16
WIDTH = 16
BAND = 4
IMAGES = 16
SECTIONS = 4


def touch_ends(values, own_key, smallest, high):
    longest = values.shape.index(max(values.shape))
    spots = []
    for shift in (0, 1):
        where = [jax.random.randint(jax.random.fold_in(own_key, axis), (), 0, length) for axis, length in enumerate(values.shape)]
        where[longest] = (where[longest] + shift) % values.shape[longest]
        spots.append(tuple(where))
    return values.at[spots[0]].set(smallest).at[spots[1]].set(high)


def levels(own_key, dims, shards, low, top_value):
    def one(dim, blocks):
        steps = jax.random.uniform(jax.random.fold_in(jax.random.fold_in(own_key, 6), dim), (blocks,), jnp.float32, low / len(shards), top_value / len(shards))
        return jnp.repeat(jnp.exp(steps), dims[dim] // blocks).reshape((-1,) + (1,) * (len(dims) - dim - 1))

    factor_of = one(*shards[0])
    for cut in shards[1:]:
        factor_of = factor_of * one(*cut)
    return factor_of


def noise(own_key, shape, scale, reach, split=(), held_as=jnp.bfloat16):
    gain = levels(own_key, shape, split, -0.22, 0.18) if split else 1.0
    values = jax.random.normal(own_key, shape, jnp.float32) * scale * gain
    return jnp.minimum(jnp.maximum(values, -reach), reach).astype(held_as)


def setup_inputs(seed: int = 0, part: int = 0) -> dict:
    keys = jax.random.split(jax.random.key(seed), 9)
    part_keys = jax.random.split(jax.random.fold_in(keys[8], part), 9)
    return {
        "activations": noise(part_keys[0], (SECTIONS, IMAGES, HEIGHT, WIDTH, CHANNELS), 1.0, 6.0, ((0, 4), (1, 4))),
        "depth_small": noise(keys[1], (SECTIONS, 3, 3, CHANNELS), 9 ** -0.5, 2.0, ((0, 4),), jnp.float32),
        "point_first": noise(keys[2], (SECTIONS, CHANNELS, CHANNELS), CHANNELS ** -0.5, 0.25, ((0, 4),)),
        "depth_large": noise(keys[3], (SECTIONS, 5, 5, CHANNELS), 25 ** -0.5, 1.25, ((0, 4),), jnp.float32),
        "point_second": noise(keys[4], (SECTIONS, CHANNELS, CHANNELS), CHANNELS ** -0.5, 0.25, ((0, 4),)),
        "head_weight": noise(keys[5], (CLASSES, CHANNELS), CHANNELS ** -0.5, 0.25),
        "offsets": touch_ends(jax.random.randint(part_keys[6], (IMAGES,), 0, WIDTH), jax.random.fold_in(part_keys[6], 1), 0, WIDTH - 1).astype(jnp.int32),
        "labels": touch_ends(jax.random.randint(part_keys[7], (IMAGES,), 0, CLASSES), jax.random.fold_in(part_keys[7], 1), 0, CLASSES - 1).astype(jnp.int32),
    }


loss_scale = 64.0


def depth_conv(inputs, kernel):
    size = kernel.shape[0]
    radius = size // 2
    height, width = inputs.shape[1], inputs.shape[2]
    padded = jnp.pad(inputs, ((0, 0), (radius, radius), (radius, radius), (0, 0)))
    result = jnp.zeros(inputs.shape, jnp.float32)
    for row_tap in range(size):
        for col_tap in range(size):
            result = result + kernel[row_tap, col_tap] * padded[:, row_tap:row_tap + height, col_tap:col_tap + width, :]
    return result


def depth_conv_t(grads, kernel):
    size = kernel.shape[0]
    radius = size // 2
    height, width = grads.shape[1], grads.shape[2]
    padded = jnp.pad(grads, ((0, 0), (radius, radius), (radius, radius), (0, 0)))
    result = jnp.zeros(grads.shape, jnp.float32)
    for row_tap in range(size):
        for col_tap in range(size):
            row_start = 2 * radius - row_tap
            col_start = 2 * radius - col_tap
            result = result + kernel[row_tap, col_tap] * padded[:, row_start:row_start + height, col_start:col_start + width, :]
    return result


def depth_conv_k(inputs, grads, size):
    radius = size // 2
    height, width = inputs.shape[1], inputs.shape[2]
    padded = jnp.pad(inputs, ((0, 0), (radius, radius), (radius, radius), (0, 0)))
    rows_out = []
    for row_tap in range(size):
        taps = []
        for col_tap in range(size):
            taps.append(jnp.sum(padded[:, row_tap:row_tap + height, col_tap:col_tap + width, :] * grads, axis=(0, 1, 2)))
        rows_out.append(jnp.stack(taps))
    return jnp.stack(rows_out)


def section_forward(section_num, activations, depth_small, point_first, depth_large, offsets):
    inputs = activations[section_num].astype(jnp.float32)
    count, height, width, chans = inputs.shape
    if section_num == 0:
        columns = jnp.arange(width, dtype=jnp.int32)
        keep = (jnp.mod(columns[None, :] - offsets[:, None], width) < BAND).astype(jnp.float32)
        inputs = inputs * keep[:, None, :, None]
    first_act = jnp.maximum(inputs, 0.0)
    first_depth = depth_conv(first_act, depth_small[section_num]).astype(jnp.bfloat16)
    first_point = jnp.dot(first_depth.reshape(-1, chans), point_first[section_num], preferred_element_type=jnp.float32)
    second_act = jnp.maximum(first_point, 0.0).astype(jnp.bfloat16).reshape(inputs.shape)
    second_depth = depth_conv(second_act.astype(jnp.float32), depth_large[section_num]).astype(jnp.bfloat16)
    return inputs, first_act, first_depth, second_act, second_depth


def reference(activations, depth_small, point_first, depth_large, point_second, head_weight, offsets, labels):
    contract_last = (((1,), (1,)), ((), ()))
    contract_first = (((0,), (0,)), ((), ()))
    last = SECTIONS - 1
    inputs, first_act, first_depth, second_act, second_depth = section_forward(last, activations, depth_small, point_first, depth_large, offsets)
    count, height, width, chans = inputs.shape
    second_point = jnp.dot(second_depth.reshape(-1, chans), point_second[last], preferred_element_type=jnp.float32)
    output = inputs + second_point.reshape(inputs.shape)
    pooled = jnp.mean(output, axis=(1, 2))
    head_float = head_weight.astype(jnp.float32)
    logits = lax.dot_general(pooled, head_float, contract_last, precision=lax.Precision.HIGHEST)
    onehot = (labels[:, None] == jnp.arange(CLASSES, dtype=jnp.int32)[None, :]).astype(jnp.float32)
    dlog = loss_scale * (logits - onehot)
    grad_pool = jnp.dot(dlog, head_float, precision=lax.Precision.HIGHEST) / (height * width)
    grad_out = jnp.broadcast_to(grad_pool[:, None, None, :], inputs.shape).astype(jnp.bfloat16)
    firsts, seconds, smalls, larges = [], [], [], []
    for section_num in range(last, -1, -1):
        inputs, first_act, first_depth, second_act, second_depth = section_forward(section_num, activations, depth_small, point_first, depth_large, offsets)
        grad_rows = grad_out.reshape(-1, chans)
        grad_depth2 = lax.dot_general(grad_rows, point_second[section_num], contract_last, preferred_element_type=jnp.float32).reshape(inputs.shape)
        seconds.append(lax.dot_general(second_depth.reshape(-1, chans), grad_rows, contract_first, preferred_element_type=jnp.float32))
        larges.append(depth_conv_k(second_act.astype(jnp.float32), grad_depth2, 5))
        back_act2 = depth_conv_t(grad_depth2, depth_large[section_num])
        grad_point1 = jnp.where(second_act > 0, back_act2, 0.0).astype(jnp.bfloat16)
        point_rows = grad_point1.reshape(-1, chans)
        grad_depth1 = lax.dot_general(point_rows, point_first[section_num], contract_last, preferred_element_type=jnp.float32).reshape(inputs.shape)
        firsts.append(lax.dot_general(first_depth.reshape(-1, chans), point_rows, contract_first, preferred_element_type=jnp.float32))
        smalls.append(depth_conv_k(first_act, grad_depth1, 3))
        back_act1 = depth_conv_t(grad_depth1, depth_small[section_num])
        grad_out = (grad_out.astype(jnp.float32) + jnp.where(inputs > 0, back_act1, 0.0)).astype(jnp.bfloat16)
    return (jnp.stack(firsts[::-1]), jnp.stack(seconds[::-1]), jnp.stack(smalls[::-1]), jnp.stack(larges[::-1]))
```

```python
import functools

import jax
import jax.numpy as jnp
from jax import lax
from jax.experimental import pallas as pl
from jax.experimental.pallas import tpu as pltpu
from jax.sharding import PartitionSpec as P

BAND = 4
LOSS_SCALE = 64.0
LANES = 128
f32 = jnp.float32
bf16 = jnp.bfloat16
contract_last = (((1,), (1,)), ((), ()))
contract_first = (((0,), (0,)), ((), ()))


def dot(a, b, dims=(((1,), (0,)), ((), ()))):
    return lax.dot_general(a, b, dims, preferred_element_type=f32)


def split_dot(values, matrix, dims):
    rows = values.shape[0]
    high = values.astype(bf16).astype(f32)
    rest = values - high
    mid = rest.astype(bf16).astype(f32)
    low = (rest - mid).astype(bf16).astype(f32)
    parts = jnp.concatenate([high, mid, low, jnp.zeros_like(low)], axis=0).astype(bf16)
    out = dot(parts, matrix, dims)
    return out[:rows] + out[rows : 2 * rows] + out[2 * rows : 3 * rows]


def kernel(
    offsets, labels, x, k3, w1, k5, w2, head,
    grad_first, grad_second, grad_small, grad_large,
    d1, a2, d2, gin, gp1, gout, tmp, s5f, s3f, s5g, s3g, pool, pool2, acc3, acc5,
    send_sem, recv_sem,
):
    section = lax.axis_index("section")
    count = lax.axis_size("section")
    images, height, width, chans = x.shape
    rows = height * width
    blocks = chans // LANES
    last = section == count - 1
    scale = 1.0 / rows

    barrier = pltpu.get_barrier_semaphore()

    @pl.when(section > 0)
    def _():
        pl.semaphore_signal(barrier, inc=1, device_id={"section": section - 1})

    @pl.when(section < count - 1)
    def _():
        pl.semaphore_signal(barrier, inc=1, device_id={"section": section + 1})

    def cols(block):
        return pl.ds(pl.multiple_of(block * LANES, LANES), LANES)

    col_index = lax.broadcasted_iota(jnp.int32, (1, width, LANES), 1)

    def shifted(value, by):
        if by == 0:
            return value
        moved = pltpu.roll(value, (-by) % width, axis=1)
        inside = (col_index + by >= 0) & (col_index + by < width)
        return jnp.where(inside, moved, 0.0)

    def fill(ref, value, size):
        radius = size // 2
        for tap in range(size):
            ref[tap, pl.ds(radius, height)] = shifted(value, tap - radius)

    def clear(ref, size):
        radius = size // 2
        zero = jnp.zeros((radius, width, LANES), f32)
        for tap in range(size):
            ref[tap, pl.ds(0, radius)] = zero
            ref[tap, pl.ds(radius + height, radius)] = zero

    def conv(ref, weights, size, block, flip):
        total = None
        for row_tap in range(size):
            for col_tap in range(size):
                r, c = row_tap, col_tap
                if flip:
                    r, c = size - 1 - r, size - 1 - c
                tap = row_tap * size + col_tap
                part = weights[pl.ds(tap, 1), cols(block)] * ref[c, pl.ds(r, height)]
                total = part if total is None else total + part
        return total

    def kept(image):
        away = col_index - offsets[image]
        away = jnp.where(away < 0, away + width, away)
        return jnp.where((away < BAND) | (section > 0), 1.0, 0.0)

    def xin(image, block):
        return x[image, :, :, cols(block)].astype(f32) * kept(image)

    clear(s5f, 5)
    clear(s3f, 3)

    @pl.loop(0, images)
    def _(n):
        @pl.loop(0, blocks)
        def _(b):
            for ref, size in ((s5g, 5), (s3g, 3)):
                clear(ref.at[n, b], size)

    @pl.loop(0, images)
    def _(n):
        @pl.loop(0, blocks)
        def _(b):
            value = xin(n, b)
            pool[n, :, cols(b)] = jnp.sum(value.reshape(rows // 8, 8, LANES), axis=0)
            fill(s3f, jnp.maximum(value, 0.0), 3)
            out = conv(s3f, k3, 3, b, False)
            d1[n, :, cols(b)] = out.reshape(rows, LANES).astype(bf16)

        a2[n] = jnp.maximum(dot(d1[n], w1[...]), 0.0).astype(bf16)

        @pl.loop(0, blocks)
        def _(b):
            value = a2[n, :, cols(b)].astype(f32).reshape(height, width, LANES)
            fill(s5f, value, 5)
            out = conv(s5f, k5, 5, b, False).reshape(rows, LANES).astype(bf16)
            d2[n, :, cols(b)] = out
            pool2[n, :, cols(b)] = jnp.sum(
                out.astype(f32).reshape(rows // 8, 8, LANES), axis=0
            )

    @pl.when(last)
    def _():
        padded, classes = -(-images // 8) * 8, head.shape[0]

        def means(ref):
            sums = [jnp.sum(ref[n], axis=0, keepdims=True) for n in range(images)]
            sums += [jnp.zeros((1, chans), f32)] * (padded - images)
            return jnp.concatenate(sums, axis=0) * scale

        pooled = means(pool) + split_dot(means(pool2), w2[...], (((1,), (0,)), ((), ())))
        logits = split_dot(pooled, head[...], contract_last)
        row_index = lax.broadcasted_iota(jnp.int32, (padded, classes), 0)
        class_index = lax.broadcasted_iota(jnp.int32, (padded, classes), 1)
        hot = jnp.zeros((padded, classes), f32)
        for n in range(images):
            hot = jnp.where((row_index == n) & (class_index == labels[n]), 1.0, hot)
        grad = split_dot(
            LOSS_SCALE * (logits - hot), head[...], (((1,), (0,)), ((), ()))
        ) * scale
        for n in range(images):
            gin[n] = jnp.broadcast_to(grad[n : n + 1], (rows, chans)).astype(bf16)

    def hand_over(n):
        return pltpu.make_async_remote_copy(
            src_ref=gout.at[n],
            dst_ref=gin.at[n],
            send_sem=send_sem.at[n],
            recv_sem=recv_sem.at[n],
            device_id={"section": jnp.maximum(section - 1, 0)},
        )

    pl.semaphore_wait(
        barrier, jnp.where(section > 0, 1, 0) + jnp.where(section < count - 1, 1, 0)
    )

    @pl.loop(0, images)
    def _(n):
        @pl.when(jnp.logical_not(last))
        def _():
            hand_over(n).wait_recv()

        tmp[...] = dot(gin[n], w2[...], contract_last)

        @pl.loop(0, blocks)
        def _(b):
            shifts = s5g.at[n, b]
            fill(shifts, tmp[:, cols(b)].reshape(height, width, LANES), 5)
            back = conv(shifts, k5, 5, b, True).reshape(rows, LANES)
            live = a2[n, :, cols(b)].astype(f32) > 0
            gp1[n, :, cols(b)] = jnp.where(live, back, 0.0).astype(bf16)

        tmp[...] = dot(gp1[n], w1[...], contract_last)

        @pl.loop(0, blocks)
        def _(b):
            shifts = s3g.at[n, b]
            fill(shifts, tmp[:, cols(b)].reshape(height, width, LANES), 3)

            @pl.when(section > 0)
            def _():
                back = conv(shifts, k3, 3, b, True)
                back = jnp.where(xin(n, b) > 0, back, 0.0).reshape(rows, LANES)
                grad = gin[n, :, cols(b)].astype(f32) + back
                gout[n, :, cols(b)] = grad.astype(bf16)

        @pl.when(section > 0)
        def _():
            hand_over(n).start()

    flat = (images * rows, chans)
    grad_second[...] = dot(d2[...].reshape(flat), gin[...].reshape(flat), contract_first)
    grad_first[...] = dot(d1[...].reshape(flat), gp1[...].reshape(flat), contract_first)

    def kernel_grad(acc, value, ref, size):
        for row_tap in range(size):
            for col_tap in range(size):
                other = ref[size - 1 - col_tap, pl.ds(size - 1 - row_tap, height)]
                part = (value * other).reshape(rows // 8, 8, LANES)
                acc[row_tap * size + col_tap] += jnp.sum(part, axis=0)

    @pl.loop(0, blocks)
    def _(b):
        acc3[...] = jnp.zeros_like(acc3)
        acc5[...] = jnp.zeros_like(acc5)

        @pl.loop(0, images)
        def _(n):
            value = a2[n, :, cols(b)].astype(f32).reshape(height, width, LANES)
            kernel_grad(acc5, value, s5g.at[n, b], 5)
            kernel_grad(acc3, jnp.maximum(xin(n, b), 0.0), s3g.at[n, b], 3)

        grad_large[:, cols(b)] = jnp.sum(acc5[...], axis=1)
        grad_small[:, cols(b)] = jnp.sum(acc3[...], axis=1)

    @pl.when(section > 0)
    def _():
        @pl.loop(0, images)
        def _(n):
            hand_over(n).wait_send()


def per_device(
    activations, depth_small, point_first, depth_large, point_second, head_weight, offsets, labels
):
    x = activations[0]
    images, height, width, chans = x.shape
    rows = height * width
    blocks = chans // LANES
    vmem = pl.BlockSpec(memory_space=pltpu.VMEM)
    smem = pl.BlockSpec(memory_space=pltpu.SMEM)
    outs = pl.pallas_call(
        kernel,
        out_shape=(
            jax.ShapeDtypeStruct((chans, chans), f32),
            jax.ShapeDtypeStruct((chans, chans), f32),
            jax.ShapeDtypeStruct((9, chans), f32),
            jax.ShapeDtypeStruct((25, chans), f32),
        ),
        in_specs=[smem, smem] + [vmem] * 6,
        out_specs=(vmem,) * 4,
        scratch_shapes=[
            pltpu.VMEM((images, rows, chans), bf16),
            pltpu.VMEM((images, rows, chans), bf16),
            pltpu.VMEM((images, rows, chans), bf16),
            pltpu.VMEM((images, rows, chans), bf16),
            pltpu.VMEM((images, rows, chans), bf16),
            pltpu.VMEM((images, rows, chans), bf16),
            pltpu.VMEM((rows, chans), f32),
            pltpu.VMEM((5, height + 4, width, LANES), f32),
            pltpu.VMEM((3, height + 2, width, LANES), f32),
            pltpu.VMEM((images, blocks, 5, height + 4, width, LANES), f32),
            pltpu.VMEM((images, blocks, 3, height + 2, width, LANES), f32),
            pltpu.VMEM((images, 8, chans), f32),
            pltpu.VMEM((images, 8, chans), f32),
            pltpu.VMEM((9, 8, LANES), f32),
            pltpu.VMEM((25, 8, LANES), f32),
            pltpu.SemaphoreType.DMA((images,)),
            pltpu.SemaphoreType.DMA((images,)),
        ],
        compiler_params=pltpu.CompilerParams(
            collective_id=0, has_side_effects=True, vmem_limit_bytes=56 << 20
        ),
        name="sections",
    )(
        offsets,
        labels,
        x,
        depth_small[0].reshape(9, chans),
        point_first[0],
        depth_large[0].reshape(25, chans),
        point_second[0],
        head_weight,
    )
    sum_first, sum_second, sum_small, sum_large = lax.psum(outs, "dp")
    return (
        sum_first[None],
        sum_second[None],
        sum_small.reshape(1, 3, 3, chans),
        sum_large.reshape(1, 5, 5, chans),
    )


def solution(mesh):
    placed = (
        P("section", ("groups", "dp"), None, None, None),
        P("section", None, None, None),
        P("section", None, None),
        P("section", None, None, None),
        P("section", None, None),
        P(),
        P(("groups", "dp")),
        P(("groups", "dp")),
    )
    return jax.shard_map(
        per_device,
        mesh=mesh,
        in_specs=placed,
        out_specs=(
            P("section", "groups", None),
            P("section", "groups", None),
            P("section", "groups", None, None),
            P("section", "groups", None, None),
        ),
        check_vma=False,
    )
```

```python
import jax
import jax.numpy as jnp
from jax import lax
from jax.experimental import pallas as pl
from jax.experimental.pallas import tpu as pltpu
from jax.sharding import PartitionSpec as P

BAND = 4
LOSS_SCALE = 64.0
LANES = 128
CHUNKS = 8
TAP_ROWS = 48
f32 = jnp.float32
bf16 = jnp.bfloat16
contract_last = (((1,), (1,)), ((), ()))
contract_first = (((0,), (0,)), ((), ()))


def dot(a, b, dims=(((1,), (0,)), ((), ()))):
    return lax.dot_general(a, b, dims, preferred_element_type=f32)


def split_dot(values, matrix, dims):
    rows = values.shape[0]
    high = values.astype(bf16).astype(f32)
    rest = values - high
    mid = rest.astype(bf16).astype(f32)
    low = (rest - mid).astype(bf16).astype(f32)
    parts = jnp.concatenate([high, mid, low, jnp.zeros_like(low)], axis=0).astype(bf16)
    out = dot(parts, matrix, dims)
    return out[:rows] + out[rows : 2 * rows] + out[2 * rows : 3 * rows]


class Line:
    def __init__(self, place, line, owner, refs, get, put):
        self.place, self.line, self.owner = place, line, owner
        self.out, self.left, self.right, self.final, self.sems = refs
        self.get, self.put = get, put

    def copy(self, k, src, dst, send, recv, step):
        return pltpu.make_async_remote_copy(
            src_ref=src.at[k],
            dst_ref=dst.at[k],
            send_sem=self.sems.at[send, k],
            recv_sem=self.sems.at[recv, k],
            device_id={"dp": jnp.clip(self.place + step, 0, self.line - 1)},
        )

    def to_right(self, k):
        return self.copy(k, self.out, self.left, 0, 3, 1)

    def to_left(self, k):
        return self.copy(k, self.out, self.right, 0, 4, -1)

    def final_left(self, k, src):
        return self.copy(k, src, self.final, 1, 5, -1)

    def final_right(self, k, src):
        return self.copy(k, src, self.final, 2, 5, 1)

    def relay(self, k):
        place, line, owner, dtype = self.place, self.line, self.owner, self.out.dtype

        def side(active, inner, arrival, source, send):
            @pl.when(active & jnp.logical_not(inner))
            def _():
                self.out[k] = self.get(k).astype(dtype)

            @pl.when(active & inner)
            def _():
                arrival(k).wait_recv()
                self.out[k] = (self.get(k) + source[k].astype(f32)).astype(dtype)

            @pl.when(active)
            def _():
                send(k).start()

        side(place < owner, place > 0, self.to_right, self.left, self.to_right)
        side(place > owner, place < line - 1, self.to_left, self.right, self.to_left)

    def total(self, k):
        line, owner, dtype = self.line, self.owner, self.out.dtype

        @pl.when(self.place == owner)
        def _():
            value = self.get(k)
            if owner > 0:
                self.to_right(k).wait_recv()
                value = value + self.left[k].astype(f32)
            if owner < line - 1:
                self.to_left(k).wait_recv()
                value = value + self.right[k].astype(f32)
            value = value.astype(dtype)
            self.out[k] = value
            if owner > 0:
                self.final_left(k, self.out).start()
            if owner < line - 1:
                self.final_right(k, self.out).start()
            self.put(k, value.astype(f32))

    def spread(self, k):
        place, line, owner = self.place, self.line, self.owner

        @pl.when(place != owner)
        def _():
            self.final_left(k, self.final).wait_recv()

        @pl.when((place < owner) & (place > 0))
        def _():
            self.final_left(k, self.final).start()

        @pl.when((place > owner) & (place < line - 1))
        def _():
            self.final_right(k, self.final).start()

        @pl.when(place != owner)
        def _():
            self.put(k, self.final[k].astype(f32))

    def drain(self, k):
        place, line, owner = self.place, self.line, self.owner

        @pl.when(place != owner)
        def _():
            self.to_right(k).wait_send()

        @pl.when((place <= owner) & (place > 0))
        def _():
            self.final_left(k, self.final).wait_send()

        @pl.when((place >= owner) & (place < line - 1))
        def _():
            self.final_right(k, self.final).wait_send()


def kernel(
    offsets, labels, x, k3, w1, k5, w2, head,
    grad_first, grad_second, grad_small, grad_large,
    d1, a2, d2, gin, gp1, gout, tmp, s5f, s3f, s5g, s3g, pool, pool2, acc3, acc5, taps,
    send_sem, recv_sem, *line_refs,
):
    section = lax.axis_index("section")
    count = lax.axis_size("section")
    images, height, width, chans = x.shape
    rows = height * width
    blocks = chans // LANES
    last = section == count - 1
    scale = 1.0 / rows

    barrier = pltpu.get_barrier_semaphore()

    @pl.when(section > 0)
    def _():
        pl.semaphore_signal(barrier, inc=1, device_id={"section": section - 1})

    @pl.when(section < count - 1)
    def _():
        pl.semaphore_signal(barrier, inc=1, device_id={"section": section + 1})

    place = lax.axis_index("dp")
    line = lax.axis_size("dp")

    @pl.when(place > 0)
    def _():
        pl.semaphore_signal(barrier, inc=1, device_id={"dp": place - 1})

    @pl.when(place < line - 1)
    def _():
        pl.semaphore_signal(barrier, inc=1, device_id={"dp": place + 1})

    def cols(block):
        return pl.ds(pl.multiple_of(block * LANES, LANES), LANES)

    col_index = lax.broadcasted_iota(jnp.int32, (1, width, LANES), 1)

    def shifted(value, by):
        if by == 0:
            return value
        moved = pltpu.roll(value, (-by) % width, axis=1)
        inside = (col_index + by >= 0) & (col_index + by < width)
        return jnp.where(inside, moved, 0.0)

    def fill(ref, value, size):
        radius = size // 2
        for tap in range(size):
            ref[tap, pl.ds(radius, height)] = shifted(value, tap - radius)

    def clear(ref, size):
        radius = size // 2
        zero = jnp.zeros((radius, width, LANES), f32)
        for tap in range(size):
            ref[tap, pl.ds(0, radius)] = zero
            ref[tap, pl.ds(radius + height, radius)] = zero

    def conv(ref, weights, size, block, flip):
        total = None
        for row_tap in range(size):
            for col_tap in range(size):
                r, c = row_tap, col_tap
                if flip:
                    r, c = size - 1 - r, size - 1 - c
                tap = row_tap * size + col_tap
                part = weights[tap, :, cols(block)] * ref[c, pl.ds(r, height)]
                total = part if total is None else total + part
        return total

    def kept(image):
        away = col_index - offsets[image]
        away = jnp.where(away < 0, away + width, away)
        return jnp.where((away < BAND) | (section > 0), 1.0, 0.0)

    def xin(image, block):
        return x[image, :, :, cols(block)].astype(f32) * kept(image)

    clear(s5f, 5)
    clear(s3f, 3)

    @pl.loop(0, images)
    def _(n):
        @pl.loop(0, blocks)
        def _(b):
            for ref, size in ((s5g, 5), (s3g, 3)):
                clear(ref.at[n, b], size)

    @pl.loop(0, images)
    def _(n):
        @pl.loop(0, blocks)
        def _(b):
            value = xin(n, b)
            pool[n, :, cols(b)] = jnp.sum(value.reshape(rows // 8, 8, LANES), axis=0)
            fill(s3f, jnp.maximum(value, 0.0), 3)
            out = conv(s3f, k3, 3, b, False)
            d1[n, :, cols(b)] = out.reshape(rows, LANES).astype(bf16)

        a2[n] = jnp.maximum(dot(d1[n], w1[...]), 0.0).astype(bf16)

        @pl.loop(0, blocks)
        def _(b):
            value = a2[n, :, cols(b)].astype(f32).reshape(height, width, LANES)
            fill(s5f, value, 5)
            out = conv(s5f, k5, 5, b, False).reshape(rows, LANES).astype(bf16)
            d2[n, :, cols(b)] = out
            pool2[n, :, cols(b)] = jnp.sum(
                out.astype(f32).reshape(rows // 8, 8, LANES), axis=0
            )

    @pl.when(last)
    def _():
        padded, classes = -(-images // 8) * 8, head.shape[0]

        def means(ref):
            sums = [jnp.sum(ref[n], axis=0, keepdims=True) for n in range(images)]
            sums += [jnp.zeros((1, chans), f32)] * (padded - images)
            return jnp.concatenate(sums, axis=0) * scale

        pooled = means(pool) + split_dot(means(pool2), w2[...], (((1,), (0,)), ((), ())))
        logits = split_dot(pooled, head[...], contract_last)
        row_index = lax.broadcasted_iota(jnp.int32, (padded, classes), 0)
        class_index = lax.broadcasted_iota(jnp.int32, (padded, classes), 1)
        hot = jnp.zeros((padded, classes), f32)
        for n in range(images):
            hot = jnp.where((row_index == n) & (class_index == labels[n]), 1.0, hot)
        grad = split_dot(
            LOSS_SCALE * (logits - hot), head[...], (((1,), (0,)), ((), ()))
        ) * scale
        for n in range(images):
            gin[n] = jnp.broadcast_to(grad[n : n + 1], (rows, chans)).astype(bf16)

    def hand_over(n):
        return pltpu.make_async_remote_copy(
            src_ref=gout.at[n],
            dst_ref=gin.at[n],
            send_sem=send_sem.at[n],
            recv_sem=recv_sem.at[n],
            device_id={"section": jnp.maximum(section - 1, 0)},
        )

    pl.semaphore_wait(
        barrier,
        jnp.where(section > 0, 1, 0)
        + jnp.where(section < count - 1, 1, 0)
        + jnp.where(place > 0, 1, 0)
        + jnp.where(place < line - 1, 1, 0),
    )

    @pl.loop(0, images)
    def _(n):
        @pl.when(jnp.logical_not(last))
        def _():
            hand_over(n).wait_recv()

        tmp[...] = dot(gin[n], w2[...], contract_last)

        @pl.loop(0, blocks)
        def _(b):
            shifts = s5g.at[n, b]
            fill(shifts, tmp[:, cols(b)].reshape(height, width, LANES), 5)
            back = conv(shifts, k5, 5, b, True).reshape(rows, LANES)
            live = a2[n, :, cols(b)].astype(f32) > 0
            gp1[n, :, cols(b)] = jnp.where(live, back, 0.0).astype(bf16)

        tmp[...] = dot(gp1[n], w1[...], contract_last)

        @pl.loop(0, blocks)
        def _(b):
            shifts = s3g.at[n, b]
            fill(shifts, tmp[:, cols(b)].reshape(height, width, LANES), 3)

            @pl.when(section > 0)
            def _():
                back = conv(shifts, k3, 3, b, True)
                back = jnp.where(xin(n, b) > 0, back, 0.0).reshape(rows, LANES)
                grad = gin[n, :, cols(b)].astype(f32) + back
                gout[n, :, cols(b)] = grad.astype(bf16)

        @pl.when(section > 0)
        def _():
            hand_over(n).start()

    flat = (images * rows, chans)
    grad_second[...] = dot(d2[...].reshape(flat), gin[...].reshape(flat), contract_first)
    grad_first[...] = dot(d1[...].reshape(flat), gp1[...].reshape(flat), contract_first)

    def kernel_grad(acc, value, ref, size):
        for row_tap in range(size):
            for col_tap in range(size):
                other = ref[size - 1 - col_tap, pl.ds(size - 1 - row_tap, height)]
                part = (value * other).reshape(rows // 8, 8, LANES)
                acc[row_tap * size + col_tap] += jnp.sum(part, axis=0)

    def kernel_grads(b):
        acc3[...] = jnp.zeros_like(acc3)
        acc5[...] = jnp.zeros_like(acc5)

        @pl.loop(0, images)
        def _(n):
            value = a2[n, :, cols(b)].astype(f32).reshape(height, width, LANES)
            kernel_grad(acc5, value, s5g.at[n, b], 5)
            kernel_grad(acc3, jnp.maximum(xin(n, b), 0.0), s3g.at[n, b], 3)

        taps[0, pl.ds(0, 25), cols(b)] = jnp.sum(acc5[...], axis=1)
        taps[0, pl.ds(32, 9), cols(b)] = jnp.sum(acc3[...], axis=1)

    middle = ((line - 1) // 2, line // 2)
    per_chunk = chans // CHUNKS

    def chunk_of(ref, k):
        return ref.at[pl.ds(pl.multiple_of(k * per_chunk, per_chunk), per_chunk)]

    def put_taps(k, value):
        for tap in range(25):
            grad_large[tap] = value[tap : tap + 1]
        for tap in range(9):
            grad_small[tap] = value[32 + tap : 33 + tap]

    def put_chunk(ref):
        def put(k, value):
            chunk_of(ref, k)[...] = value

        return put

    lines = (
        Line(place, line, middle[0], line_refs[0:5],
             lambda k: chunk_of(grad_second, k)[...], put_chunk(grad_second)),
        Line(place, line, middle[1], line_refs[5:10],
             lambda k: chunk_of(grad_first, k)[...], put_chunk(grad_first)),
    )
    tap_line = Line(place, line, middle[0], line_refs[10:15], lambda k: taps[k], put_taps)

    @pl.loop(0, CHUNKS + 3)
    def _(step):
        @pl.when(step < CHUNKS)
        def _():
            for each in lines:
                each.relay(step)

        @pl.when(step < blocks)
        def _():
            kernel_grads(step)

        @pl.when(step == blocks)
        def _():
            tap_line.relay(0)

        @pl.when((step >= 1) & (step < CHUNKS + 1))
        def _():
            for each in lines:
                each.total(step - 1)

        @pl.when(step == blocks + 1)
        def _():
            tap_line.total(0)

        @pl.when(step >= 3)
        def _():
            for each in lines:
                each.spread(step - 3)

        @pl.when(step == blocks + 3)
        def _():
            tap_line.spread(0)

    tap_line.drain(0)

    @pl.loop(0, CHUNKS)
    def _(k):
        for each in lines:
            each.drain(k)

    @pl.when(section > 0)
    def _():
        @pl.loop(0, images)
        def _(n):
            hand_over(n).wait_send()


def per_device(
    activations, depth_small, point_first, depth_large, point_second, head_weight, offsets, labels
):
    x = activations[0]
    images, height, width, chans = x.shape
    rows = height * width
    blocks = chans // LANES
    vmem = pl.BlockSpec(memory_space=pltpu.VMEM)
    smem = pl.BlockSpec(memory_space=pltpu.SMEM)

    def line_scratch(chunks, length, dtype):
        return [pltpu.VMEM((chunks, length, chans), dtype)] * 4 + [
            pltpu.SemaphoreType.DMA((6, chunks))
        ]

    sum_first, sum_second, sum_small, sum_large = pl.pallas_call(
        kernel,
        out_shape=(
            jax.ShapeDtypeStruct((chans, chans), f32),
            jax.ShapeDtypeStruct((chans, chans), f32),
            jax.ShapeDtypeStruct((9, 1, chans), f32),
            jax.ShapeDtypeStruct((25, 1, chans), f32),
        ),
        in_specs=[smem, smem] + [vmem] * 6,
        out_specs=(vmem,) * 4,
        scratch_shapes=[
            pltpu.VMEM((images, rows, chans), bf16),
            pltpu.VMEM((images, rows, chans), bf16),
            pltpu.VMEM((images, rows, chans), bf16),
            pltpu.VMEM((images, rows, chans), bf16),
            pltpu.VMEM((images, rows, chans), bf16),
            pltpu.VMEM((images, rows, chans), bf16),
            pltpu.VMEM((rows, chans), f32),
            pltpu.VMEM((5, height + 4, width, LANES), f32),
            pltpu.VMEM((3, height + 2, width, LANES), f32),
            pltpu.VMEM((images, blocks, 5, height + 4, width, LANES), f32),
            pltpu.VMEM((images, blocks, 3, height + 2, width, LANES), f32),
            pltpu.VMEM((images, 8, chans), f32),
            pltpu.VMEM((images, 8, chans), f32),
            pltpu.VMEM((9, 8, LANES), f32),
            pltpu.VMEM((25, 8, LANES), f32),
            pltpu.VMEM((1, TAP_ROWS, chans), f32),
            pltpu.SemaphoreType.DMA((images,)),
            pltpu.SemaphoreType.DMA((images,)),
            *line_scratch(CHUNKS, chans // CHUNKS, bf16),
            *line_scratch(CHUNKS, chans // CHUNKS, bf16),
            *line_scratch(1, TAP_ROWS, f32),
        ],
        compiler_params=pltpu.CompilerParams(
            collective_id=0, has_side_effects=True, vmem_limit_bytes=56 << 20
        ),
        name="sections",
    )(
        offsets,
        labels,
        x,
        depth_small[0].reshape(9, 1, chans),
        point_first[0],
        depth_large[0].reshape(25, 1, chans),
        point_second[0],
        head_weight,
    )
    return (
        sum_first[None],
        sum_second[None],
        sum_small.reshape(1, 3, 3, chans),
        sum_large.reshape(1, 5, 5, chans),
    )


def solution(mesh):
    placed = (
        P("section", ("groups", "dp"), None, None, None),
        P("section", None, None, None),
        P("section", None, None),
        P("section", None, None, None),
        P("section", None, None),
        P(),
        P(("groups", "dp")),
        P(("groups", "dp")),
    )
    return jax.shard_map(
        per_device,
        mesh=mesh,
        in_specs=placed,
        out_specs=(
            P("section", "groups", None),
            P("section", "groups", None),
            P("section", "groups", None, None),
            P("section", "groups", None, None),
        ),
        check_vma=False,
    )
```

```python
import jax
import jax.numpy as jnp
from jax import lax
from jax.experimental import pallas as pl
from jax.experimental.pallas import tpu as pltpu
from jax.sharding import PartitionSpec as P

BAND = 4
LOSS_SCALE = 64.0
LANES = 128
CHUNKS = 8
LAG = 1
UNITS = 4
TAP_ROWS = 48
f32 = jnp.float32
bf16 = jnp.bfloat16
contract_last = (((1,), (1,)), ((), ()))
contract_first = (((0,), (0,)), ((), ()))


def dot(a, b, dims=(((1,), (0,)), ((), ()))):
    return lax.dot_general(a, b, dims, preferred_element_type=f32)


def split_dot(values, matrix, dims):
    rows = values.shape[0]
    high = values.astype(bf16).astype(f32)
    rest = values - high
    mid = rest.astype(bf16).astype(f32)
    low = (rest - mid).astype(bf16).astype(f32)
    parts = jnp.concatenate([high, mid, low, jnp.zeros_like(low)], axis=0).astype(bf16)
    out = dot(parts, matrix, dims)
    return out[:rows] + out[rows : 2 * rows] + out[2 * rows : 3 * rows]


class Line:
    def __init__(self, place, line, owner, refs, get, put):
        self.place, self.line, self.owner = place, line, owner
        self.out, self.left, self.right, self.final, self.sems = refs
        self.get, self.put = get, put

    def copy(self, k, src, dst, send, recv, step):
        return pltpu.make_async_remote_copy(
            src_ref=src.at[k],
            dst_ref=dst.at[k],
            send_sem=self.sems.at[send, k],
            recv_sem=self.sems.at[recv, k],
            device_id={"dp": jnp.clip(self.place + step, 0, self.line - 1)},
        )

    def to_right(self, k):
        return self.copy(k, self.out, self.left, 0, 3, 1)

    def to_left(self, k):
        return self.copy(k, self.out, self.right, 0, 4, -1)

    def final_left(self, k, src):
        return self.copy(k, src, self.final, 1, 5, -1)

    def final_right(self, k, src):
        return self.copy(k, src, self.final, 2, 5, 1)

    def advance(self, phase, step, chunks):
        place, line, owner = self.place, self.line, self.owner
        outer = jnp.where(place < owner, place, line - 1 - place)
        apart = jnp.where(place < owner, owner - place, place - owner)
        meet = max(owner, line - 1 - owner)
        if phase == 0:
            k, active, act = step - LAG * outer, place != owner, self.relay
        elif phase == 1:
            k, active, act = step - LAG * meet, place == owner, self.total
        else:
            k, active, act = step - LAG * (meet + apart), place != owner, self.spread

        @pl.when(active & (k >= 0) & (k < chunks))
        def _():
            act(k)

    def relay(self, k):
        place, line, owner, dtype = self.place, self.line, self.owner, self.out.dtype

        def side(active, inner, arrival, source, send):
            @pl.when(active & jnp.logical_not(inner))
            def _():
                self.out[k] = self.get(k).astype(dtype)

            @pl.when(active & inner)
            def _():
                arrival(k).wait_recv()
                self.out[k] = (self.get(k) + source[k].astype(f32)).astype(dtype)

            @pl.when(active)
            def _():
                send(k).start()

        side(place < owner, place > 0, self.to_right, self.left, self.to_right)
        side(place > owner, place < line - 1, self.to_left, self.right, self.to_left)

    def total(self, k):
        line, owner, dtype = self.line, self.owner, self.out.dtype

        @pl.when(self.place == owner)
        def _():
            value = self.get(k)
            if owner > 0:
                self.to_right(k).wait_recv()
                value = value + self.left[k].astype(f32)
            if owner < line - 1:
                self.to_left(k).wait_recv()
                value = value + self.right[k].astype(f32)
            value = value.astype(dtype)
            self.out[k] = value
            if owner > 0:
                self.final_left(k, self.out).start()
            if owner < line - 1:
                self.final_right(k, self.out).start()
            self.put(k, value.astype(f32))

    def spread(self, k):
        place, line, owner = self.place, self.line, self.owner

        @pl.when(place != owner)
        def _():
            self.final_left(k, self.final).wait_recv()

        @pl.when((place < owner) & (place > 0))
        def _():
            self.final_left(k, self.final).start()

        @pl.when((place > owner) & (place < line - 1))
        def _():
            self.final_right(k, self.final).start()

        @pl.when(place != owner)
        def _():
            self.put(k, self.final[k].astype(f32))

    def drain(self, k):
        place, line, owner = self.place, self.line, self.owner

        @pl.when(place != owner)
        def _():
            self.to_right(k).wait_send()

        @pl.when((place <= owner) & (place > 0))
        def _():
            self.final_left(k, self.final).wait_send()

        @pl.when((place >= owner) & (place < line - 1))
        def _():
            self.final_right(k, self.final).wait_send()


def kernel(
    offsets, labels, x, k3, w1, k5, w2, head,
    grad_first, grad_second, grad_small, grad_large,
    d1, a2, d2, gin, gp1, gout, tmp, s5f, s3f, s5g, s3g, pool, pool2, acc3, acc5, taps,
    send_sem, recv_sem, *line_refs,
):
    section = lax.axis_index("section")
    count = lax.axis_size("section")
    images, height, width, chans = x.shape
    rows = height * width
    blocks = chans // LANES
    last = section == count - 1
    scale = 1.0 / rows

    barrier = pltpu.get_barrier_semaphore()

    @pl.when(section > 0)
    def _():
        pl.semaphore_signal(barrier, inc=1, device_id={"section": section - 1})

    @pl.when(section < count - 1)
    def _():
        pl.semaphore_signal(barrier, inc=1, device_id={"section": section + 1})

    place = lax.axis_index("dp")
    line = lax.axis_size("dp")

    @pl.when(place > 0)
    def _():
        pl.semaphore_signal(barrier, inc=1, device_id={"dp": place - 1})

    @pl.when(place < line - 1)
    def _():
        pl.semaphore_signal(barrier, inc=1, device_id={"dp": place + 1})

    def cols(block):
        return pl.ds(pl.multiple_of(block * LANES, LANES), LANES)

    col_index = lax.broadcasted_iota(jnp.int32, (1, width, LANES), 1)

    def shifted(value, by):
        if by == 0:
            return value
        moved = pltpu.roll(value, (-by) % width, axis=1)
        inside = (col_index + by >= 0) & (col_index + by < width)
        return jnp.where(inside, moved, 0.0)

    def fill(ref, value, size):
        radius = size // 2
        for tap in range(size):
            ref[tap, pl.ds(radius, height)] = shifted(value, tap - radius)

    def clear(ref, size):
        radius = size // 2
        zero = jnp.zeros((radius, width, LANES), f32)
        for tap in range(size):
            ref[tap, pl.ds(0, radius)] = zero
            ref[tap, pl.ds(radius + height, radius)] = zero

    def conv(ref, weights, size, block, flip):
        total = None
        for row_tap in range(size):
            for col_tap in range(size):
                r, c = row_tap, col_tap
                if flip:
                    r, c = size - 1 - r, size - 1 - c
                tap = row_tap * size + col_tap
                part = weights[tap, :, cols(block)] * ref[c, pl.ds(r, height)]
                total = part if total is None else total + part
        return total

    def kept(image):
        away = col_index - offsets[image]
        away = jnp.where(away < 0, away + width, away)
        return jnp.where((away < BAND) | (section > 0), 1.0, 0.0)

    def xin(image, block):
        return x[image, :, :, cols(block)].astype(f32) * kept(image)

    clear(s5f, 5)
    clear(s3f, 3)

    @pl.loop(0, images)
    def _(n):
        @pl.loop(0, blocks)
        def _(b):
            for ref, size in ((s5g, 5), (s3g, 3)):
                clear(ref.at[n, b], size)

    @pl.loop(0, images)
    def _(n):
        @pl.loop(0, blocks)
        def _(b):
            value = xin(n, b)
            pool[n, :, cols(b)] = jnp.sum(value.reshape(rows // 8, 8, LANES), axis=0)
            fill(s3f, jnp.maximum(value, 0.0), 3)
            out = conv(s3f, k3, 3, b, False)
            d1[n, :, cols(b)] = out.reshape(rows, LANES).astype(bf16)

        a2[n] = jnp.maximum(dot(d1[n], w1[...]), 0.0).astype(bf16)

        @pl.loop(0, blocks)
        def _(b):
            value = a2[n, :, cols(b)].astype(f32).reshape(height, width, LANES)
            fill(s5f, value, 5)
            out = conv(s5f, k5, 5, b, False).reshape(rows, LANES).astype(bf16)
            d2[n, :, cols(b)] = out
            pool2[n, :, cols(b)] = jnp.sum(
                out.astype(f32).reshape(rows // 8, 8, LANES), axis=0
            )

    @pl.when(last)
    def _():
        padded, classes = -(-images // 8) * 8, head.shape[0]

        def means(ref):
            sums = [jnp.sum(ref[n], axis=0, keepdims=True) for n in range(images)]
            sums += [jnp.zeros((1, chans), f32)] * (padded - images)
            return jnp.concatenate(sums, axis=0) * scale

        pooled = means(pool) + split_dot(means(pool2), w2[...], (((1,), (0,)), ((), ())))
        logits = split_dot(pooled, head[...], contract_last)
        row_index = lax.broadcasted_iota(jnp.int32, (padded, classes), 0)
        class_index = lax.broadcasted_iota(jnp.int32, (padded, classes), 1)
        hot = jnp.zeros((padded, classes), f32)
        for n in range(images):
            hot = jnp.where((row_index == n) & (class_index == labels[n]), 1.0, hot)
        grad = split_dot(
            LOSS_SCALE * (logits - hot), head[...], (((1,), (0,)), ((), ()))
        ) * scale
        for n in range(images):
            gin[n] = jnp.broadcast_to(grad[n : n + 1], (rows, chans)).astype(bf16)

    def hand_over(n):
        return pltpu.make_async_remote_copy(
            src_ref=gout.at[n],
            dst_ref=gin.at[n],
            send_sem=send_sem.at[n],
            recv_sem=recv_sem.at[n],
            device_id={"section": jnp.maximum(section - 1, 0)},
        )

    pl.semaphore_wait(
        barrier,
        jnp.where(section > 0, 1, 0)
        + jnp.where(section < count - 1, 1, 0)
        + jnp.where(place > 0, 1, 0)
        + jnp.where(place < line - 1, 1, 0),
    )

    @pl.loop(0, images)
    def _(n):
        @pl.when(jnp.logical_not(last))
        def _():
            hand_over(n).wait_recv()

        tmp[...] = dot(gin[n], w2[...], contract_last)

        @pl.loop(0, blocks)
        def _(b):
            shifts = s5g.at[n, b]
            fill(shifts, tmp[:, cols(b)].reshape(height, width, LANES), 5)
            back = conv(shifts, k5, 5, b, True).reshape(rows, LANES)
            live = a2[n, :, cols(b)].astype(f32) > 0
            gp1[n, :, cols(b)] = jnp.where(live, back, 0.0).astype(bf16)

        tmp[...] = dot(gp1[n], w1[...], contract_last)

        @pl.loop(0, blocks)
        def _(b):
            shifts = s3g.at[n, b]
            fill(shifts, tmp[:, cols(b)].reshape(height, width, LANES), 3)

            @pl.when(section > 0)
            def _():
                back = conv(shifts, k3, 3, b, True)
                back = jnp.where(xin(n, b) > 0, back, 0.0).reshape(rows, LANES)
                grad = gin[n, :, cols(b)].astype(f32) + back
                gout[n, :, cols(b)] = grad.astype(bf16)

        @pl.when(section > 0)
        def _():
            hand_over(n).start()

    flat = (images * rows, chans)
    grad_second[...] = dot(d2[...].reshape(flat), gin[...].reshape(flat), contract_first)
    grad_first[...] = dot(d1[...].reshape(flat), gp1[...].reshape(flat), contract_first)

    def kernel_grad(acc, value, ref, size):
        for row_tap in range(size):
            for col_tap in range(size):
                other = ref[size - 1 - col_tap, pl.ds(size - 1 - row_tap, height)]
                part = (value * other).reshape(rows // 8, 8, LANES)
                acc[row_tap * size + col_tap] += jnp.sum(part, axis=0)

    def kernel_grads(unit):
        b, n = unit // images, unit % images

        @pl.when(n == 0)
        def _():
            acc3[...] = jnp.zeros_like(acc3)
            acc5[...] = jnp.zeros_like(acc5)

        value = a2[n, :, cols(b)].astype(f32).reshape(height, width, LANES)
        kernel_grad(acc5, value, s5g.at[n, b], 5)
        kernel_grad(acc3, jnp.maximum(xin(n, b), 0.0), s3g.at[n, b], 3)

        @pl.when(n == images - 1)
        def _():
            taps[b, pl.ds(0, 25)] = jnp.sum(acc5[...], axis=1)
            taps[b, pl.ds(32, 9)] = jnp.sum(acc3[...], axis=1)

    middle = ((line - 1) // 2, line // 2)
    per_chunk = chans // CHUNKS

    def chunk_of(ref, k):
        return ref.at[pl.ds(pl.multiple_of(k * per_chunk, per_chunk), per_chunk)]

    def put_taps(k, value):
        for tap in range(25):
            grad_large[tap, :, cols(k)] = value[tap : tap + 1]
        for tap in range(9):
            grad_small[tap, :, cols(k)] = value[32 + tap : 33 + tap]

    def put_chunk(ref):
        def put(k, value):
            chunk_of(ref, k)[...] = value

        return put

    lines = (
        Line(place, line, middle[0], line_refs[0:5],
             lambda k: chunk_of(grad_second, k)[...], put_chunk(grad_second)),
        Line(place, line, middle[1], line_refs[5:10],
             lambda k: chunk_of(grad_first, k)[...], put_chunk(grad_first)),
    )
    tap_line = Line(place, line, middle[0], line_refs[10:15], lambda k: taps[k], put_taps)

    busy = -(-blocks * images // UNITS)
    chunks = CHUNKS

    @pl.loop(0, max(chunks, busy + blocks) + LAG * line)
    def _(step):
        for phase in range(3):
            for each in lines:
                each.advance(phase, step, chunks)
            tap_line.advance(phase, step - busy, blocks)
            if phase == 0:

                @pl.when(step < busy)
                def _():
                    @pl.loop(0, UNITS)
                    def _(part):
                        kernel_grads(step * UNITS + part)

    @pl.loop(0, blocks)
    def _(k):
        tap_line.drain(k)

    @pl.loop(0, CHUNKS)
    def _(k):
        for each in lines:
            each.drain(k)

    @pl.when(section > 0)
    def _():
        @pl.loop(0, images)
        def _(n):
            hand_over(n).wait_send()


def per_device(
    activations, depth_small, point_first, depth_large, point_second, head_weight, offsets, labels
):
    x = activations[0]
    images, height, width, chans = x.shape
    rows = height * width
    blocks = chans // LANES
    vmem = pl.BlockSpec(memory_space=pltpu.VMEM)
    smem = pl.BlockSpec(memory_space=pltpu.SMEM)

    link = bf16 if lax.axis_size("dp") <= 4 else f32

    def line_scratch(chunks, length, wide, dtype):
        return [pltpu.VMEM((chunks, length, wide), dtype)] * 4 + [
            pltpu.SemaphoreType.DMA((6, chunks))
        ]

    sum_first, sum_second, sum_small, sum_large = pl.pallas_call(
        kernel,
        out_shape=(
            jax.ShapeDtypeStruct((chans, chans), f32),
            jax.ShapeDtypeStruct((chans, chans), f32),
            jax.ShapeDtypeStruct((9, 1, chans), f32),
            jax.ShapeDtypeStruct((25, 1, chans), f32),
        ),
        in_specs=[smem, smem] + [vmem] * 6,
        out_specs=(vmem,) * 4,
        scratch_shapes=[
            pltpu.VMEM((images, rows, chans), bf16),
            pltpu.VMEM((images, rows, chans), bf16),
            pltpu.VMEM((images, rows, chans), bf16),
            pltpu.VMEM((images, rows, chans), bf16),
            pltpu.VMEM((images, rows, chans), bf16),
            pltpu.VMEM((images, rows, chans), bf16),
            pltpu.VMEM((rows, chans), f32),
            pltpu.VMEM((5, height + 4, width, LANES), f32),
            pltpu.VMEM((3, height + 2, width, LANES), f32),
            pltpu.VMEM((images, blocks, 5, height + 4, width, LANES), f32),
            pltpu.VMEM((images, blocks, 3, height + 2, width, LANES), f32),
            pltpu.VMEM((images, 8, chans), f32),
            pltpu.VMEM((images, 8, chans), f32),
            pltpu.VMEM((9, 8, LANES), f32),
            pltpu.VMEM((25, 8, LANES), f32),
            pltpu.VMEM((blocks, TAP_ROWS, LANES), f32),
            pltpu.SemaphoreType.DMA((images,)),
            pltpu.SemaphoreType.DMA((images,)),
            *line_scratch(CHUNKS, chans // CHUNKS, chans, link),
            *line_scratch(CHUNKS, chans // CHUNKS, chans, link),
            *line_scratch(blocks, TAP_ROWS, LANES, f32),
        ],
        compiler_params=pltpu.CompilerParams(
            collective_id=0, has_side_effects=True, vmem_limit_bytes=56 << 20
        ),
        name="sections",
    )(
        offsets,
        labels,
        x,
        depth_small[0].reshape(9, 1, chans),
        point_first[0],
        depth_large[0].reshape(25, 1, chans),
        point_second[0],
        head_weight,
    )
    return (
        sum_first[None],
        sum_second[None],
        sum_small.reshape(1, 3, 3, chans),
        sum_large.reshape(1, 5, 5, chans),
    )


def solution(mesh):
    placed = (
        P("section", ("groups", "dp"), None, None, None),
        P("section", None, None, None),
        P("section", None, None),
        P("section", None, None, None),
        P("section", None, None),
        P(),
        P(("groups", "dp")),
        P(("groups", "dp")),
    )
    return jax.shard_map(
        per_device,
        mesh=mesh,
        in_specs=placed,
        out_specs=(
            P("section", "groups", None),
            P("section", "groups", None),
            P("section", "groups", None, None),
            P("section", "groups", None, None),
        ),
        check_vma=False,
    )
```
